256 devices in a mesh: dp: 16 (over z_lo, y), expert: 16 (over z_hi, x, core).
Axes of the slice: x: 4, y: 4, z: 8 (z_hi: 2, z_lo: 4; z = z_hi * 4 + z_lo), core: 2. Of those that a mesh axis runs over, the one named last changes fastest.
Arguments:
- tokens: bfloat16 [32768, 2048], P(('dp', 'expert')), may hold values from -24 to 24
- routes: int32 [32768, 4], P(('dp', 'expert')), may hold values from 0 to 31, all different within a row; in each aligned block of 128 rows (0 to 127, 128 to 255, ...) at most 24 rows name the same one
- combine: bfloat16 [32768, 4], P(('dp', 'expert')), may hold values from 0.049804688 to 1
- out_cotangent: bfloat16 [32768, 2048], P(('dp', 'expert')), may hold values from -6 to 6
- gate_weight: bfloat16 [32, 2048, 384], P('expert'), may hold values from -0.125 to 0.125
- up_weight: bfloat16 [32, 2048, 384], P('expert'), may hold values from -0.125 to 0.125
- down_weight: bfloat16 [32, 2048, 384], P('expert'), may hold values from -0.3125 to 0.3125
Outputs:
- token_grads: bfloat16 [32768, 2048], P(('dp', 'expert'))
- combine_grads: bfloat16 [32768, 4], P(('dp', 'expert'))
- gate_grads: float32 [32, 2048, 384], P('expert', 'dp')
- up_grads: float32 [32, 2048, 384], P('expert', 'dp')
- down_grads: float32 [32, 2048, 384], P('expert', 'dp')
The draws below stay inside these ranges and needn't reach their ends.
Inputs may be any that keep to these rules, and one draw needn't show every extreme that they name: `routes`: each token names 4 different experts; among the 128 tokens of one device no expert is named more than 24 times, and in some devices an expert is named exactly 24 times.
All inputs are finite; a program needn't handle non-finite values.
Results may differ from the reference program's by a relative error of at most 0.017.
Values may be sent and summed in bfloat16 or wider, within the bound.
No kernel may reach another device: no remote copies, remote signals or barrier semaphores. Data moves between devices by JAX's collectives and lax.ppermute only.
A program may use at most 128 MiB of HBM per device.

```python
import math
import jax
import jax.numpy as jnp
import numpy as np
from jax import lax

D = 2048
FF = 384
TOP = 4
TOK_DEV = 128
EXPERTS = 32
CAP = 24
TOKENS = 32768
N_DP = 16
N_EXPERT = 16


def spiked(entries, own_key, source, target, parts, factor):
    owner, partner = [(jnp.arange(entries.shape[axis_at]) // (entries.shape[axis_at] // parts)).reshape([-1 if axis == axis_at else 1 for axis in range(entries.ndim)]) for axis_at in (source, target)]
    chosen = jax.random.permutation(own_key, parts)[partner]
    strong = (owner == chosen) | (owner == (partner + parts // 2) % parts)
    return jnp.where(strong, factor * entries, entries)


def level_of(stream_key, shape, split, smallest, largest):
    def one(dim, parts):
        heights = jax.random.uniform(jax.random.fold_in(jax.random.fold_in(stream_key, 6), dim), (parts,), jnp.float32, smallest / len(split), largest / len(split))
        return jnp.repeat(jnp.exp(heights), shape[dim] // parts).reshape((-1,) + (1,) * (len(shape) - dim - 1))

    level = one(*split[0])
    for cut in split[1:]:
        level = level * one(*cut)
    return level


def routed_block(rng, own, number, rows, amount, top, limit, skew):
    order = jax.random.permutation(rng, amount)
    packed, ordinary = load_shares(amount, rows * top, limit, skew, True), load_shares(amount, rows * top, limit, skew, False)
    places = jnp.arange(amount)

    def named(tallies, rotation):
        used = int((tallies > 0).sum())
        fixed = max(1, used // 4)
        passed = fixed + (places - fixed + rotation * (used - fixed)) % max(1, amount - fixed)
        return jnp.zeros((amount,), jnp.int32).at[order[jnp.where(places < fixed, places, passed)]].set(jnp.asarray(tallies, jnp.int32))

    tallies = jnp.where(number % 4 == 0, named(packed, number // 4), named(ordinary, number - number // 4 - 1))
    mixed = jax.random.permutation(jax.random.fold_in(own, 3), amount)
    source_of, taker = mixed[0:amount // 2 * 2:2], mixed[1:amount // 2 * 2:2]
    slack = jnp.minimum(tallies[source_of] - 1, limit - tallies[taker]) // 2
    slack = jnp.where((source_of == order[0]) | (taker == order[0]) | (tallies[taker] == 0), 0, jnp.maximum(slack, 0))
    passed = jax.random.randint(jax.random.fold_in(own, 4), (amount // 2,), 0, 1 << 20) % (slack + 1)
    tallies = tallies.at[source_of].add(-passed).at[taker].add(passed)
    labels = jnp.searchsorted(jnp.cumsum(tallies), jnp.arange(rows * top), side="right").astype(jnp.int32)
    table = labels.reshape(top, rows).T
    table = table[jax.random.permutation(jax.random.fold_in(own, 1), rows)]
    rotation = jax.random.randint(jax.random.fold_in(own, 2), (rows, 1), 0, top)
    return jnp.take_along_axis(table, (jnp.arange(top)[None, :] + rotation) % top, axis=1)


def load_shares(count, total, bound, slope, full):
    portions = [(1 << 20) // math.isqrt(grade ** slope) + 1 for grade in range(1, count + 1)]
    largest = bound if full else min(bound, max(-(-total // count), total * portions[0] // sum(portions)))
    least = 1 if total - largest >= count - 1 else 0
    given, spare = [largest] + [least] * (count - 1), total - largest - least * (count - 1)
    while spare > 0:
        free = [i for i in range(1, count) if given[i] < largest] or [i for i in range(1, count) if given[i] < bound]
        whole, budget = sum([portions[i] for i in free]), spare
        for i in free:
            addition = min(bound - given[i], max(1, budget * portions[i] // whole), spare)
            given[i] = given[i] + addition
            spare = spare - addition
    return np.array(given)


def gaussian(own_key, extent, scale, reach, cuts=(), kind=jnp.bfloat16):
    entries = scale * jax.random.normal(own_key, extent, jnp.float32)
    if cuts:
        entries = entries * level_of(own_key, extent, cuts, -0.22, 0.18)
    return jnp.clip(entries, -reach, reach).astype(kind)


def bell_draw_with(rng, dims, scale, bound, pieces, heavy, kind=jnp.bfloat16):
    array = scale * jax.random.normal(rng, dims, jnp.float32)
    if pieces:
        array = array * level_of(rng, dims, pieces, -0.22, 0.18)
    return jnp.clip(spiked(array, jax.random.fold_in(rng, 3), *heavy), -bound, bound).astype(kind)


def setup_inputs(seed: int = 0) -> dict:
    splits = jax.random.split(jax.random.key(seed), 8)
    tokens = bell_draw_with(splits[0], (TOKENS, D), 1.0, 24.0, ((0, 256),), (0, 1, 256, 6.0))
    routes_keys = jax.random.split(jax.random.fold_in(splits[1], 1), TOKENS // TOK_DEV)
    routes_turns = jax.random.permutation(jax.random.fold_in(splits[1], 3), TOKENS // TOK_DEV)
    routes = jax.vmap(lambda own, number: routed_block(jax.random.fold_in(splits[1], 2), own, number, TOK_DEV, EXPERTS, TOP, CAP, 2))(routes_keys, routes_turns).reshape((TOKENS, TOP))
    combine = jnp.clip(jnp.exp(math.log(1.0) - 2.9996462 * jax.random.uniform(splits[2], (TOKENS, TOP), jnp.float32) ** level_of(splits[2], (TOKENS, TOP), ((0, 256),), -0.2, 0.2)), 0.049804688, 1.0).astype(jnp.bfloat16)
    out_cotangent = bell_draw_with(splits[3], (TOKENS, D), 0.25, 6.0, ((0, 256),), (0, 1, 256, 6.0))
    gate_weight = gaussian(splits[4], (EXPERTS, D, FF), D ** -0.5, 0.125, ((0, 16),))
    up_weight = gaussian(splits[5], (EXPERTS, D, FF), D ** -0.5, 0.125, ((0, 16),))
    down_weight = gaussian(splits[6], (EXPERTS, D, FF), FF ** -0.5, 0.3125, ((0, 16),))
    return dict(tokens=tokens, routes=routes, combine=combine, out_cotangent=out_cotangent, gate_weight=gate_weight, up_weight=up_weight, down_weight=down_weight)


def build_table(routes):
    devices = N_DP * N_EXPERT
    route_count = TOK_DEV * TOP
    expert_ids = jnp.arange(EXPERTS, dtype=jnp.int32)
    flat_ids = routes.reshape(devices, route_count)
    onehot = (flat_ids[:, :, None] == expert_ids[None, None, :]).astype(jnp.int32)
    before = jnp.cumsum(onehot, axis=1) - onehot
    rank_ids = jnp.sum(before * onehot, axis=2)
    slot_ids = flat_ids * CAP + rank_ids
    source = jnp.arange(devices, dtype=jnp.int32)[:, None] + jnp.zeros((1, route_count), jnp.int32)
    position = source * route_count + jnp.arange(route_count, dtype=jnp.int32)[None, :]
    filled = jnp.full((devices, EXPERTS * CAP), TOKENS * TOP, jnp.int32)
    filled = filled.at[source, slot_ids].set(position)
    return filled.reshape(devices, EXPERTS, CAP)


def group_sum(left, right):
    left_groups = left.astype(jnp.float32).reshape(N_DP, N_EXPERT * CAP, left.shape[1])
    right_groups = right.astype(jnp.float32).reshape(N_DP, N_EXPERT * CAP, right.shape[1])
    partial_sums = jnp.einsum("grd,grf->gdf", left_groups, right_groups).astype(jnp.bfloat16)
    partial_sums = lax.optimization_barrier(partial_sums)
    return jnp.sum(partial_sums.astype(jnp.float32), axis=0)


def reference(tokens, routes, combine, out_cotangent, gate_weight, up_weight, down_weight):
    owners = jnp.transpose(build_table(routes), (1, 0, 2))
    zero_row = jnp.zeros((1, D), jnp.bfloat16)
    token_pad = jnp.concatenate([tokens, zero_row], 0)
    cot_pad = jnp.concatenate([out_cotangent, zero_row], 0)
    weight_pad = jnp.concatenate([combine.reshape(-1), jnp.zeros((1,), jnp.bfloat16)], 0)

    def expert_step(carry, inputs):
        token_acc, score_acc = carry
        owner_ids, gate_w, up_w, down_w = inputs
        owner_ids = owner_ids.reshape(-1)
        row_ids = owner_ids // TOP
        token_rows = token_pad[row_ids]
        gate_act = jnp.dot(token_rows, gate_w, preferred_element_type=jnp.float32)
        up_act = jnp.dot(token_rows, up_w, preferred_element_type=jnp.float32)
        gate_sig = jax.nn.sigmoid(gate_act)
        hidden = (gate_act * gate_sig * up_act).astype(jnp.bfloat16)
        expert_out = jnp.dot(hidden, down_w.T, preferred_element_type=jnp.float32).astype(jnp.bfloat16)
        cot_rows = cot_pad[row_ids]
        weight = weight_pad[owner_ids].astype(jnp.float32)
        scores = jnp.sum(cot_rows.astype(jnp.float32) * expert_out.astype(jnp.float32), axis=1)
        out_cot = (weight[:, None] * cot_rows.astype(jnp.float32)).astype(jnp.bfloat16)
        hidden_cot = jnp.dot(out_cot, down_w, preferred_element_type=jnp.float32)
        gate_cot = (hidden_cot * up_act * gate_sig * (1.0 + gate_act * (1.0 - gate_sig))).astype(jnp.bfloat16)
        up_cot = (hidden_cot * gate_act * gate_sig).astype(jnp.bfloat16)
        rows_cot = (jnp.dot(gate_cot, gate_w.T, preferred_element_type=jnp.float32)
                    + jnp.dot(up_cot, up_w.T, preferred_element_type=jnp.float32)).astype(jnp.bfloat16)
        gate_part = group_sum(token_rows, gate_cot)
        up_part = group_sum(token_rows, up_cot)
        down_part = group_sum(out_cot, hidden)
        token_acc = token_acc.at[row_ids].add(rows_cot.astype(jnp.float32))
        score_acc = score_acc.at[owner_ids].set(scores)
        return (token_acc, score_acc), (gate_part, up_part, down_part)

    start = (jnp.zeros((TOKENS + 1, D), jnp.float32), jnp.zeros((TOKENS * TOP + 1,), jnp.float32))
    (token_acc, score_acc), (gate_grads, up_grads, down_grads) = lax.scan(
        expert_step, start, (owners, gate_weight, up_weight, down_weight))
    token_grads = token_acc[:TOKENS].astype(jnp.bfloat16)
    combine_grads = score_acc[:TOKENS * TOP].reshape(TOKENS, TOP).astype(jnp.bfloat16)
    return token_grads, combine_grads, gate_grads, up_grads, down_grads
```

```python
import functools
import jax
import jax.numpy as jnp
from jax import lax
from jax.experimental import pallas as pl
from jax.experimental.pallas import tpu as pltpu
from jax.sharding import PartitionSpec as P

CAP = 24
F32, BF16 = jnp.float32, jnp.bfloat16
QS = [(rel, flip) for rel in range(4) for flip in range(2)]


def perm_q(rel, flip):
    return [
        (e, (e & 8) | (((((e >> 1) & 3) + rel) & 3) << 1) | ((e & 1) ^ flip)) for e in range(16)
    ]


PERM_H = [(e, e ^ 8) for e in range(16)]


def perm_y(step):
    return [(d, (d & 12) | ((d + step) & 3)) for d in range(16)]


def perm_z(mask):
    return [(d, d ^ (mask << 2)) for d in range(16)]


def dims(a, b):
    return (((a,), (b,)), ((), ()))


def dot(a, b, ca, cb):
    return lax.dot_general(a, b, dims(ca, cb), preferred_element_type=F32)


def ranks(hit):
    before = lax.broadcasted_iota(jnp.int32, (128, 128), 0)
    after = lax.broadcasted_iota(jnp.int32, (128, 128), 1)
    upper = jnp.where(before < after, 1.0, 0.0).astype(BF16)
    return dot(hit.astype(BF16), upper, 1, 0)


def match(meta_ref, ids):
    hit = jnp.zeros(ids.shape, F32)
    weight = jnp.zeros(ids.shape, F32)
    for k in range(4):
        same = ids == meta_ref[k : k + 1, :]
        hit = hit + jnp.where(same, 1.0, 0.0)
        weight = weight + jnp.where(same, meta_ref[4 + k : 5 + k, :], 0.0)
    return hit, weight


def selection(pos_ref, meta_ref):
    h, x, c = pos_ref[0], pos_ref[1], pos_ref[2]
    row = lax.broadcasted_iota(jnp.int32, (16, 128), 0)
    ids = h * 16 + ((x + (row >> 2)) & 3) * 4 + ((c ^ ((row >> 1) & 1)) * 2) + (row & 1)
    hit, weight = match(meta_ref, ids.astype(F32))
    count = ranks(hit)
    slot = lax.broadcasted_iota(jnp.int32, (16, CAP, 128), 1).astype(F32)
    picked = jnp.where(hit > 0.0, count, -1.0)[:, None, :] == slot
    return picked, weight


def one_hot(picked):
    return jnp.where(picked, 1.0, 0.0).reshape(16 * CAP, 128).astype(BF16)


def weighted_hot(picked, weight):
    return jnp.where(picked, weight[:, None, :], 0.0).reshape(16 * CAP, 128).astype(BF16)


def pack_own(pos_ref, meta_ref, tok_ref, cot_ref, *outs):
    picked, weight = selection(pos_ref, meta_ref)
    rows = dot(one_hot(picked), tok_ref[...], 1, 0)
    cots = dot(weighted_hot(picked, weight), cot_ref[...], 1, 0)
    for q in range(8):
        outs[q][0] = rows[q * 48 : q * 48 + 48].astype(BF16)
        outs[q][1] = cots[q * 48 : q * 48 + 48].astype(BF16)


def pack_one(scaled, pos_ref, meta_ref, src_ref, *outs):
    picked, weight = selection(pos_ref, meta_ref)
    mat = weighted_hot(picked, weight) if scaled else one_hot(picked)
    rows = dot(mat, src_ref[...], 1, 0)
    for q in range(8):
        outs[q][...] = rows[q * 48 : q * 48 + 48].astype(BF16)


def gather_rows(own, par, dst):
    def half(b, j):
        block = own[b][0] if b < 8 else par[b - 8][...]
        return block.astype(F32)[j * CAP : j * CAP + CAP]

    for p in range(8):
        for j in range(2):
            pair = jnp.concatenate([half(2 * p, j), half(2 * p + 1, j)], 0)
            dst[j, p * 48 : p * 48 + 48, :] = pair.astype(BF16)


def forward(*refs):
    own, par = refs[:8], refs[8:16]
    wg, wu, rows, hid, fac_g, fac_u = refs[16:]
    gather_rows(own, par, rows)
    for j in range(2):
        gate = dot(rows[j], wg[j], 1, 0)
        up = dot(rows[j], wu[j], 1, 0)
        sig = lax.logistic(gate)
        hid[j] = (gate * sig * up).astype(BF16)
        fac_g[j] = up * sig * (1.0 + gate * (1.0 - sig))
        fac_u[j] = gate * sig


def spread(pos_ref, res_ref, outs, j):
    y, z = pos_ref[3], pos_ref[4]
    for rel in range(4):
        for m in range(4):
            first = pl.multiple_of(((z ^ m) * 4 + ((y + rel) & 3)) * 128, 128)
            part = res_ref[pl.ds(first, 128), :].astype(BF16)
            if rel < 2:
                outs[rel][m, j] = part
            elif rel == 2:
                outs[2 + m // 2][m % 2, j] = part
            else:
                outs[4][m, j] = part


def backward(pos_ref, *refs):
    own, par = refs[:8], refs[8:16]
    wd, hid, fac_g, fac_u = refs[16:20]
    score, cots, outs = refs[20], refs[21], refs[22:27]
    rows, res = refs[27:]
    h, x, c = pos_ref[0], pos_ref[1], pos_ref[2]
    gather_rows(own, par, rows)
    score[...] = jnp.zeros(score.shape, F32)
    lane = lax.broadcasted_iota(jnp.int32, (16, CAP, 128), 2)
    slot = lax.broadcasted_iota(jnp.int32, (16, CAP, 128), 1)
    for j in range(2):
        hc = dot(rows[j], wd[j], 1, 0)
        sums = jnp.sum(hid[j].astype(F32) * hc, axis=1, keepdims=True).reshape(16, CAP, 1)
        table = jnp.sum(jnp.where(lane == slot, sums, 0.0), axis=1)
        for b in range(16):
            rel, flip = QS[b % 8]
            to = (h ^ (b // 8)) * 8 + ((x - rel) & 3) * 2 + (c ^ flip)
            score[to, j : j + 1, :] = table[b : b + 1, :]
        cots[j, :, :384] = (hc * fac_g[j]).astype(BF16)
        cots[j, :, 384:] = (hc * fac_u[j]).astype(BF16)
        res[...] = dot(rows[j], hid[j], 0, 0)
        spread(pos_ref, res, outs, j)


def weight_grads(pos_ref, rows, cots, *refs):
    outs, res = refs[:10], refs[10]
    for j in range(2):
        for part in range(2):
            res[...] = dot(rows[j], cots[j, :, part * 384 : part * 384 + 384], 0, 0)
            spread(pos_ref, res, outs[part * 5 : part * 5 + 5], j)


def input_grads(cots, wg, wu, *refs):
    outs, res = refs[:8], refs[8]
    for j in range(2):
        res[j] = dot(cots[j, :, :384], wg[j], 1, 1) + dot(cots[j, :, 384:], wu[j], 1, 1)
    for b in range(16):
        both = [res[j, b * CAP : b * CAP + CAP, :] for j in range(2)]
        outs[b % 8][b // 8] = jnp.concatenate(both, 0).astype(BF16)


def collect(pos_ref, meta_ref, blocks):
    picked, _ = selection(pos_ref, meta_ref)
    rows = jnp.concatenate([block[0] for block in blocks], 0)
    return dot(one_hot(picked), rows, 0, 0)


def unpack_par(pos_ref, meta_ref, *refs):
    refs[8][...] = collect(pos_ref, meta_ref, refs[:8]).astype(BF16)


def unpack_own(pos_ref, meta_ref, *refs):
    score, other, grads, scores_out = refs[8:]
    total = collect(pos_ref, meta_ref, refs[:8]) + other[...].astype(F32)
    grads[...] = total.astype(BF16)
    scores_out[...] = jnp.zeros(scores_out.shape, F32)
    row = lax.broadcasted_iota(jnp.int32, (16, 128), 0)
    sums = [jnp.zeros((1, 128), F32)] * 4
    for j in range(2):
        ids = (row * 2 + j).astype(F32)
        hit, _ = match(meta_ref, ids)
        count = jnp.where(hit > 0.0, ranks(hit), -1.0)
        table = score[:, j, :]
        mine = jnp.zeros((16, 128), F32)
        for r in range(CAP):
            mine = mine + jnp.where(count == float(r), table[:, r : r + 1], 0.0)
        for k in range(4):
            chosen = jnp.where(ids == meta_ref[k : k + 1, :], mine, 0.0)
            sums[k] = sums[k] + jnp.sum(chosen, axis=0, keepdims=True)
    for k in range(4):
        scores_out[k : k + 1, :] = sums[k] / meta_ref[4 + k : 5 + k, :]


SMEM = pl.BlockSpec(memory_space=pltpu.SMEM)


def whole(shape):
    return pl.BlockSpec(shape, lambda i: (0,) * len(shape))


def half_of(n):
    return pl.BlockSpec((1, 48, 2048), lambda i: (n, 0, 0))


def call(body, in_specs, outs, scratch=(), name=None):
    return pl.pallas_call(
        body,
        grid=(1,),
        in_specs=in_specs,
        out_specs=[whole(s.shape) for s in outs],
        out_shape=outs,
        scratch_shapes=list(scratch),
        name=name,
    )


def arr(shape, kind=BF16):
    return jax.ShapeDtypeStruct(shape, kind)


META, TOK, BLK, ROWS, WGT = (8, 128), (128, 2048), (48, 2048), (2, 384, 2048), (2, 2048, 384)
ACT = (2, 384, 384)
PAIR = (2, 48, 2048)
CHUNKS = [(4, 2, 128, 384), (4, 2, 128, 384), (2, 2, 128, 384), (2, 2, 128, 384), (4, 2, 128, 384)]


def spread_over(blocks, sign):
    return [
        blocks[q]
        if QS[q] == (0, 0)
        else lax.ppermute(blocks[q], "expert", perm_q(sign * QS[q][0], QS[q][1]))
        for q in range(8)
    ]


def reduce_dp(parts):
    own, right, far_a, far_b, left = parts
    got_a = lax.ppermute(far_a, "dp", perm_y(1)).astype(F32)
    got_b = lax.ppermute(far_b, "dp", perm_y(-1)).astype(F32)
    right = jnp.concatenate([(right[:2].astype(F32) + got_a).astype(BF16), right[2:]], 0)
    left = jnp.concatenate([left[:2], (left[2:].astype(F32) + got_b).astype(BF16)], 0)
    from_left = lax.ppermute(right, "dp", perm_y(1))
    from_right = lax.ppermute(left, "dp", perm_y(-1))
    sums = [
        own[m].astype(F32) + from_left[m].astype(F32) + from_right[m].astype(F32) for m in range(4)
    ]
    total = sums[0]
    for m in range(1, 4):
        total = total + lax.ppermute(sums[m].astype(BF16), "dp", perm_z(m)).astype(F32)
    return total


def local(tokens, routes, combine, out_cotangent, gate_weight, up_weight, down_weight):
    e, d = lax.axis_index("expert"), lax.axis_index("dp")
    pos = jnp.stack([e >> 3, (e >> 1) & 3, e & 1, d & 3, d >> 2]).astype(jnp.int32)
    meta = jnp.concatenate([routes.astype(F32).T, combine.astype(F32).T], 0)
    meta_par = lax.ppermute(meta, "expert", PERM_H)
    tok_par = lax.ppermute(tokens, "expert", PERM_H)
    cot_par = lax.ppermute(out_cotangent, "expert", PERM_H)

    own = call(
        pack_own,
        [SMEM, whole(META), whole(TOK), whole(TOK)],
        [arr(PAIR)] * 8,
        name="pack_own",
    )(pos, meta, tokens, out_cotangent)
    own = spread_over(own, 1)
    pack = lambda scaled, name: call(
        functools.partial(pack_one, scaled),
        [SMEM, whole(META), whole(TOK)],
        [arr(BLK)] * 8,
        name=name,
    )
    par_t = spread_over(pack(False, "pack_tok")(pos, meta_par, tok_par), 1)
    par_c = spread_over(pack(True, "pack_cot")(pos, meta_par, cot_par), 1)

    rows, hid, fac_g, fac_u = call(
        forward,
        [half_of(0)] * 8 + [whole(BLK)] * 8 + [whole(WGT)] * 2,
        [arr(ROWS), arr(ACT), arr(ACT, F32), arr(ACT, F32)],
        name="forward",
    )(*own, *par_t, gate_weight, up_weight)
    score, cots, *down = call(
        backward,
        [SMEM] + [half_of(1)] * 8 + [whole(BLK)] * 8 + [whole(WGT)] + [whole(ACT)] * 3,
        [arr((16, 8, 128), F32), arr((2, 384, 768))] + [arr(s) for s in CHUNKS],
        [pltpu.VMEM(ROWS, BF16), pltpu.VMEM((2048, 384), F32)],
        name="backward",
    )(pos, *own, *par_c, down_weight, hid, fac_g, fac_u)
    score = lax.all_to_all(score, "expert", split_axis=0, concat_axis=0, tiled=True)
    back = call(
        input_grads,
        [whole((2, 384, 768)), whole(WGT), whole(WGT)],
        [arr(PAIR)] * 8,
        [pltpu.VMEM(ROWS, F32)],
        name="input_grads",
    )(cots, gate_weight, up_weight)
    back = spread_over(back, -1)
    parts = call(
        weight_grads,
        [SMEM, whole(ROWS), whole((2, 384, 768))],
        [arr(s) for s in CHUNKS * 2],
        [pltpu.VMEM((2048, 384), F32)],
        name="weight_grads",
    )(pos, rows, cots)
    down_grads = reduce_dp(down)
    gate_grads = reduce_dp(parts[:5])
    up_grads = reduce_dp(parts[5:])
    (other,) = call(
        unpack_par, [SMEM, whole(META)] + [half_of(1)] * 8, [arr(TOK)], name="unpack_par"
    )(pos, meta_par, *back)
    other = lax.ppermute(other, "expert", PERM_H)
    token_grads, scores = call(
        unpack_own,
        [SMEM, whole(META)] + [half_of(0)] * 8 + [whole((16, 8, 128)), whole(TOK)],
        [arr(TOK), arr(META, F32)],
        name="unpack_own",
    )(pos, meta, *back, score, other)
    combine_grads = scores[:4].T.astype(BF16)
    return (token_grads, combine_grads, gate_grads, up_grads, down_grads)


def solution(mesh):
    tok, wgt = P(("dp", "expert"), None), P("expert", None, None)
    return jax.shard_map(
        local,
        mesh=mesh,
        in_specs=(tok, tok, tok, tok, wgt, wgt, wgt),
        out_specs=(tok, tok) + (P("expert", "dp", None),) * 3,
        check_vma=False,
    )
```

```python
import functools
import jax
import jax.numpy as jnp
from jax import lax
from jax.experimental import pallas as pl
from jax.experimental.pallas import tpu as pltpu
from jax.sharding import PartitionSpec as P

CAP = 24
F32, BF16 = jnp.float32, jnp.bfloat16
QS = [(rel, flip) for rel in range(4) for flip in range(2)]


def perm_q(rel, flip):
    return [
        (e, (e & 8) | (((((e >> 1) & 3) + rel) & 3) << 1) | ((e & 1) ^ flip)) for e in range(16)
    ]


PERM_H = [(e, e ^ 8) for e in range(16)]


def perm_y(step):
    return [(d, (d & 12) | ((d + step) & 3)) for d in range(16)]


def perm_z(mask):
    return [(d, d ^ (mask << 2)) for d in range(16)]


def dims(a, b):
    return (((a,), (b,)), ((), ()))


def dot(a, b, ca, cb):
    return lax.dot_general(a, b, dims(ca, cb), preferred_element_type=F32)


def ranks(hit):
    before = lax.broadcasted_iota(jnp.int32, (128, 128), 0)
    after = lax.broadcasted_iota(jnp.int32, (128, 128), 1)
    upper = jnp.where(before < after, 1.0, 0.0).astype(BF16)
    return dot(hit.astype(BF16), upper, 1, 0)


def by_token(cols):
    eye = lax.broadcasted_iota(jnp.int32, (128, 128), 0) == lax.broadcasted_iota(
        jnp.int32, (128, 128), 1
    )
    return dot(cols, jnp.where(eye, 1.0, 0.0).astype(BF16), 0, 0)


def selection(pos_ref, cols):
    h, x, c = pos_ref[0], pos_ref[1], pos_ref[2]
    meta = by_token(cols)
    row = lax.broadcasted_iota(jnp.int32, (16, 128), 0)
    ids = h * 16 + ((x + (row >> 2)) & 3) * 4 + ((c ^ ((row >> 1) & 1)) * 2) + (row & 1)
    ids = ids.astype(F32)
    hit = jnp.zeros(ids.shape, F32)
    weight = jnp.zeros(ids.shape, F32)
    for k in range(4):
        same = ids == meta[k : k + 1, :]
        hit = hit + jnp.where(same, 1.0, 0.0)
        weight = weight + jnp.where(same, meta[4 + k : 5 + k, :], 0.0)
    count = jnp.where(hit > 0.0, ranks(hit), -1.0)
    slot = lax.broadcasted_iota(jnp.int32, (16, CAP, 128), 1).astype(F32)
    picked = count[:, None, :] == slot
    return picked, weight, ids, meta


def one_hot(picked):
    return jnp.where(picked, 1.0, 0.0).reshape(16 * CAP, 128).astype(BF16)


def weighted_hot(picked, weight):
    return jnp.where(picked, weight[:, None, :], 0.0).reshape(16 * CAP, 128).astype(BF16)


def pack_own(pos_ref, tok_ref, cot_ref, *outs):
    picked, weight, _, _ = selection(pos_ref, tok_ref[:, 2048:])
    rows = dot(one_hot(picked), tok_ref[:, :2048], 1, 0)
    cots = dot(weighted_hot(picked, weight), cot_ref[...], 1, 0)
    for q in range(8):
        outs[q][0] = rows[q * 48 : q * 48 + 48].astype(BF16)
        outs[q][1] = cots[q * 48 : q * 48 + 48].astype(BF16)


def pack_tok(pos_ref, tok_ref, *outs):
    picked, _, _, _ = selection(pos_ref, tok_ref[:, 2048:])
    rows = dot(one_hot(picked), tok_ref[:, :2048], 1, 0)
    for q in range(8):
        outs[q][...] = rows[q * 48 : q * 48 + 48].astype(BF16)


def pack_cot(pos_ref, cols_ref, cot_ref, *outs):
    picked, weight, _, _ = selection(pos_ref, cols_ref[...])
    rows = dot(weighted_hot(picked, weight), cot_ref[...], 1, 0)
    for q in range(8):
        outs[q][...] = rows[q * 48 : q * 48 + 48].astype(BF16)


def gather_rows(own, par, dst):
    def half(b, j):
        block = own[b][0] if b < 8 else par[b - 8][...]
        return block.astype(F32)[j * CAP : j * CAP + CAP]

    for p in range(8):
        for j in range(2):
            pair = jnp.concatenate([half(2 * p, j), half(2 * p + 1, j)], 0)
            dst[j, p * 48 : p * 48 + 48, :] = pair.astype(BF16)


def forward(*refs):
    own, par = refs[:8], refs[8:16]
    wg, wu, rows, hid, fac_g, fac_u = refs[16:]
    gather_rows(own, par, rows)
    for j in range(2):
        gate = dot(rows[j], wg[j], 1, 0)
        up = dot(rows[j], wu[j], 1, 0)
        sig = lax.logistic(gate)
        hid[j] = (gate * sig * up).astype(BF16)
        fac_g[j] = up * sig * (1.0 + gate * (1.0 - sig))
        fac_u[j] = gate * sig


def spread(pos_ref, res_ref, outs, j):
    y, z = pos_ref[3], pos_ref[4]
    own_a, own_b, plus, minus, right_a, left_b = outs
    for i, m in enumerate(ORDER):
        targets = [
            (own_a, i) if i < 2 else (own_b, i - 2),
            (right_a, i) if i < 2 else (plus, i),
            (plus, i) if i < 2 else (minus, i - 2),
            (minus, i + 2) if i < 2 else (left_b, i - 2),
        ]
        for rel, (out, at) in enumerate(targets):
            first = pl.multiple_of(((z ^ m) * 4 + ((y + rel) & 3)) * 128, 128)
            out[at, j] = res_ref[pl.ds(first, 128), :].astype(BF16)


def backward(pos_ref, *refs):
    own, par = refs[:8], refs[8:16]
    wd, hid, fac_g, fac_u = refs[16:20]
    score, cots, outs = refs[20], refs[21], refs[22:28]
    rows, res = refs[28:]
    gather_rows(own, par, rows)
    lane = lax.broadcasted_iota(jnp.int32, (384, 128), 1)
    for j in range(2):
        hc = dot(rows[j], wd[j], 1, 0)
        sums = jnp.sum(hid[j].astype(F32) * hc, axis=1, keepdims=True)
        high = sums.astype(BF16).astype(F32)
        score[j] = jnp.where(lane == 0, high, jnp.where(lane == 1, sums - high, 0.0))
        cots[j, :, :384] = (hc * fac_g[j]).astype(BF16)
        cots[j, :, 384:] = (hc * fac_u[j]).astype(BF16)
        res[...] = dot(rows[j], hid[j], 0, 0)
        spread(pos_ref, res, outs, j)


def weight_grads(pos_ref, rows, cots, *refs):
    outs, res = refs[:12], refs[12]
    for part in range(2):
        for j in range(2):
            res[...] = dot(rows[j], cots[j, :, part * 384 : part * 384 + 384], 0, 0)
            spread(pos_ref, res, outs[part * 6 : part * 6 + 6], j)


def input_grads(cots, score, wg, wu, *refs):
    outs, res = refs[:8], refs[8]
    for j in range(2):
        res[j, :, :2048] = dot(cots[j, :, :384], wg[j], 1, 1) + dot(cots[j, :, 384:], wu[j], 1, 1)
        res[j, :, 2048:] = score[j]
    for b in range(16):
        both = [res[j, b * CAP : b * CAP + CAP, :] for j in range(2)]
        outs[b % 8][b // 8] = jnp.concatenate(both, 0).astype(BF16)


def collect(pos_ref, cols, blocks):
    picked, _, ids, meta = selection(pos_ref, cols)
    rows = jnp.concatenate([block[0] for block in blocks], 0)
    total = dot(one_hot(picked), rows[:, :2048], 0, 0)
    sums = []
    for k in range(4):
        mine = jnp.where(ids == meta[k : k + 1, :], 1.0, 0.0)
        got = dot(weighted_hot(picked, mine), rows[:, 2048:], 0, 0)
        sums.append(got[:, 0:1] + got[:, 1:2])
    return total, sums


def unpack_par(pos_ref, cols_ref, *refs):
    total, sums = collect(pos_ref, cols_ref[...], refs[:8])
    refs[8][:, :2048] = total.astype(BF16)
    lane = lax.broadcasted_iota(jnp.int32, (128, 128), 1)
    ext = jnp.zeros((128, 128), F32)
    for k in range(4):
        high = sums[k].astype(BF16).astype(F32)
        ext = jnp.where(lane == 2 * k, high, ext)
        ext = jnp.where(lane == 2 * k + 1, sums[k] - high, ext)
    refs[8][:, 2048:] = ext.astype(BF16)


def unpack_own(pos_ref, cols_ref, *refs):
    other, grads, scores = refs[8:]
    total, sums = collect(pos_ref, cols_ref[...], refs[:8])
    grads[...] = (total + other[:, :2048].astype(F32)).astype(BF16)
    ext = other[:, 2048:].astype(F32)
    cols = cols_ref[...].astype(F32)
    lane = lax.broadcasted_iota(jnp.int32, (128, 128), 1)
    out = jnp.zeros((128, 128), F32)
    for k in range(4):
        whole_sum = sums[k] + ext[:, 2 * k : 2 * k + 1] + ext[:, 2 * k + 1 : 2 * k + 2]
        out = jnp.where(lane == k, whole_sum / cols[:, 4 + k : 5 + k], out)
    scores[...] = out[:, :4].astype(BF16)


SMEM = pl.BlockSpec(memory_space=pltpu.SMEM)


def whole(shape):
    return pl.BlockSpec(shape, lambda i: (0,) * len(shape))


def half_of(n, width=2048):
    return pl.BlockSpec((1, 48, width), lambda i: (n, 0, 0))


COLS = pl.BlockSpec((128, 128), lambda i: (0, 16))


def call(body, in_specs, outs, scratch=(), name=None):
    return pl.pallas_call(
        body,
        grid=(1,),
        in_specs=in_specs,
        out_specs=[whole(s.shape) for s in outs],
        out_shape=outs,
        scratch_shapes=list(scratch),
        name=name,
    )


def arr(shape, kind=BF16):
    return jax.ShapeDtypeStruct(shape, kind)


TOK, EXT, BLK, ROWS, WGT = (128, 2048), (128, 2176), (48, 2048), (2, 384, 2048), (2, 2048, 384)
ACT, COT, SCORE = (2, 384, 384), (2, 384, 768), (2, 384, 128)
PAIR, BACK = (2, 48, 2048), (2, 48, 2176)
ORDER = [1, 3, 0, 2]
CHUNKS = [(n, 2, 128, 384) for n in (2, 2, 4, 4, 2, 2)]


def spread_over(blocks, sign):
    return [
        blocks[q]
        if QS[q] == (0, 0)
        else lax.ppermute(blocks[q], "expert", perm_q(sign * QS[q][0], QS[q][1]))
        for q in range(8)
    ]


def reduce_dp(parts):
    own_a, own_b, plus, minus, right_a, left_b = parts
    got_p = lax.ppermute(plus, "dp", perm_y(1))
    got_m = lax.ppermute(minus, "dp", perm_y(-1))
    right_a = (right_a.astype(F32) + got_p[:2].astype(F32)).astype(BF16)
    left_b = (left_b.astype(F32) + got_m[:2].astype(F32)).astype(BF16)
    got_a = lax.ppermute(right_a, "dp", perm_y(1)).astype(F32)
    got_b = lax.ppermute(left_b, "dp", perm_y(-1)).astype(F32)
    sum_a = own_a.astype(F32) + got_m[2:].astype(F32) + got_a
    sum_b = own_b.astype(F32) + got_p[2:].astype(F32) + got_b
    near = lax.ppermute(sum_a.astype(BF16), "dp", perm_z(1)).astype(F32)
    across = (sum_b[1] + near[1]).astype(BF16)
    return sum_b[0] + near[0] + lax.ppermute(across, "dp", perm_z(2)).astype(F32)


def local(tokens, routes, combine, out_cotangent, gate_weight, up_weight, down_weight):
    e, d = lax.axis_index("expert"), lax.axis_index("dp")
    pos = jnp.stack([e >> 3, (e >> 1) & 3, e & 1, d & 3, d >> 2]).astype(jnp.int32)
    cols = [routes.astype(BF16), combine, jnp.zeros((128, 120), BF16)]
    tok = jnp.concatenate([tokens] + cols, 1)
    tok_par = lax.ppermute(tok, "expert", PERM_H)
    cot_par = lax.ppermute(out_cotangent, "expert", PERM_H)

    own = call(
        pack_own, [SMEM, whole(EXT), whole(TOK)], [arr(PAIR)] * 8, name="pack_own"
    )(pos, tok, out_cotangent)
    own = spread_over(own, 1)
    par_t = call(pack_tok, [SMEM, whole(EXT)], [arr(BLK)] * 8, name="pack_tok")(pos, tok_par)
    par_t = spread_over(par_t, 1)
    par_c = call(pack_cot, [SMEM, COLS, whole(TOK)], [arr(BLK)] * 8, name="pack_cot")(
        pos, tok_par, cot_par
    )
    par_c = spread_over(par_c, 1)

    rows, hid, fac_g, fac_u = call(
        forward,
        [half_of(0)] * 8 + [whole(BLK)] * 8 + [whole(WGT)] * 2,
        [arr(ROWS), arr(ACT), arr(ACT, F32), arr(ACT, F32)],
        name="forward",
    )(*own, *par_t, gate_weight, up_weight)
    score, cots, *down = call(
        backward,
        [SMEM] + [half_of(1)] * 8 + [whole(BLK)] * 8 + [whole(WGT)] + [whole(ACT)] * 3,
        [arr(SCORE, F32), arr(COT)] + [arr(s) for s in CHUNKS],
        [pltpu.VMEM(ROWS, BF16), pltpu.VMEM((2048, 384), F32)],
        name="backward",
    )(pos, *own, *par_c, down_weight, hid, fac_g, fac_u)
    parts = call(
        weight_grads,
        [SMEM, whole(ROWS), whole(COT)],
        [arr(s) for s in CHUNKS * 2],
        [pltpu.VMEM((2048, 384), F32)],
        name="weight_grads",
    )(pos, rows, cots)
    later, _ = lax.optimization_barrier((cots, parts[0]))
    back = call(
        input_grads,
        [whole(COT), whole(SCORE), whole(WGT), whole(WGT)],
        [arr(BACK)] * 8,
        [pltpu.VMEM((2, 384, 2176), F32)],
        name="input_grads",
    )(later, score, gate_weight, up_weight)
    back = spread_over(back, -1)
    down_grads = reduce_dp(down)
    gate_grads = reduce_dp(parts[:6])
    up_grads = reduce_dp(parts[6:])
    (other,) = call(
        unpack_par, [SMEM, COLS] + [half_of(1, 2176)] * 8, [arr(EXT)], name="unpack_par"
    )(pos, tok_par, *back)
    other = lax.ppermute(other, "expert", PERM_H)
    token_grads, combine_grads = call(
        unpack_own,
        [SMEM, COLS] + [half_of(0, 2176)] * 8 + [whole(EXT)],
        [arr(TOK), arr((128, 4))],
        name="unpack_own",
    )(pos, tok, *back, other)
    return (token_grads, combine_grads, gate_grads, up_grads, down_grads)


def solution(mesh):
    tok, wgt = P(("dp", "expert"), None), P("expert", None, None)
    return jax.shard_map(
        local,
        mesh=mesh,
        in_specs=(tok, tok, tok, tok, wgt, wgt, wgt),
        out_specs=(tok, tok) + (P("expert", "dp", None),) * 3,
        check_vma=False,
    )
```
